32 devices in a mesh: grp: 4 (over x, core), dom: 8 (over z, y).
Axes of the slice: x: 2, y: 2, z: 4, core: 2. Of those that a mesh axis runs over, the one named last changes fastest.
Arguments:
- cell_index: int32 [3, 65536], P(None, ('grp', 'dom')), may hold values from 0 to 255, as said below
- offsets: float32 [3, 65536], P(None, ('grp', 'dom')), may hold values from -0.5 to 0.5
- species: int32 [65536], P(('grp', 'dom')), may hold values from 0 to 7
- pair_blocks: int32 [128, 2], P(('grp', 'dom')), may hold values from 0 to 47, as said below
- counts: int32 [32], P(('grp', 'dom')), may hold values from 1 to 4, as said below
- background: float32 [256, 256, 256], P('dom', 'grp'), may hold values from -0.12 to 0.12
- species_embed: float32 [8, 256], replicated, may hold values from -6 to 6
- neighbour_embed: float32 [8, 256], replicated, may hold values from -6 to 6
- w_radial: float32 [8, 256], replicated, may hold values from -2 to 2
- w_hidden: bfloat16 [256, 256], replicated, may hold values from -0.375 to 0.375
- w_charge: bfloat16 [256], replicated, may hold values from -0.375 to 0.375
- w_energy: bfloat16 [256], replicated, may hold values from -0.375 to 0.375
Outputs:
- site_energy: float32 [65536], P(('grp', 'dom'))
- electric_field: float32 [3, 65536], P(None, ('grp', 'dom'))
- charges: float32 [65536], P(('grp', 'dom'))
The draws below stay inside these ranges and needn't reach their ends.
Inputs may be any that keep to these rules, and one draw needn't show every extreme that they name: `cell_index`: atoms of domain k = g * 8 + d (atoms k * 2048 on) have a first index in [32 d, 32 d + 32) and a second in [64 g, 64 g + 64). Atom block b of a domain lies in second-index tile b mod 4 of width 64 / 4 and third-index tile b // 4 of width 256 / 4. `pair_blocks`: the i block is one of the domain's 16 blocks; the j block indexes the 48 extended blocks and lies in the same or an adjacent tile of its domain. `counts`: some device has exactly 4 live slots in every draw.
All inputs are finite; a program needn't handle non-finite values.
Results may differ from the reference program's by a relative error of at most 0.0003.
The reference program's roundings to bfloat16 on the way count: a program that leaves them out, or rounds other values in their place, can miss the bound.
Values sent between devices are 32-bit elements; how exact they have to be, the bound alone decides.
A program may use at most 128 MiB of HBM per device.

```python
import math
import jax
import jax.numpy as jnp
import numpy as np
from jax import lax

G = 256
D = 256
NBASIS = 8
NSPEC = 8
BLOCK = 128
A_DEV = 2048
PB_CAP = 4
NB = 16
SLAB = 32
QY = 64
ATOMS = 65536
PAIRS = 128
N_GRP = 4
N_DOM = 8


def draw_cell_index(key, part):
    atom_ids = jnp.arange(ATOMS, dtype=jnp.int32)
    device_ids = atom_ids // A_DEV
    group_ids = device_ids // N_DOM
    domain_ids = device_ids % N_DOM
    block_ids = atom_ids % A_DEV // BLOCK
    tiles_z = NB // 4
    tile_y_len = QY // 4
    tile_z_len = G // tiles_z
    key_x, key_y, key_z = jax.random.split(jax.random.fold_in(key, 11), 3)
    coord_x = SLAB * domain_ids + jax.random.randint(key_x, (ATOMS,), 0, SLAB)
    coord_y = QY * group_ids + block_ids % 4 * tile_y_len + jax.random.randint(key_y, (ATOMS,), 0, tile_y_len)
    coord_z = block_ids // 4 * tile_z_len + jax.random.randint(key_z, (ATOMS,), 0, tile_z_len)
    return jnp.stack([coord_x, coord_y, coord_z], axis=0).astype(jnp.int32)


def draw_pair_blocks(key, part):
    key_i, key_side, key_dy, key_dz = jax.random.split(jax.random.fold_in(key, 23), 4)
    block_i = jax.random.randint(key_i, (PAIRS,), 0, NB)
    side_ids = jax.random.randint(key_side, (PAIRS,), 0, 3)
    delta_y = jax.random.randint(key_dy, (PAIRS,), -1, 2)
    delta_z = jax.random.randint(key_dz, (PAIRS,), -1, 2)
    tiles_z = NB // 4
    tile_y = jnp.clip(block_i % 4 + delta_y, 0, 3)
    tile_z = (block_i // 4 + delta_z + tiles_z) % tiles_z
    block_j = side_ids * NB + tile_z * 4 + tile_y
    return jnp.stack([block_i, block_j], axis=1).astype(jnp.int32)


def draw_counts(key, part):
    device_total = PAIRS // PB_CAP
    key_a, key_b, key_top = jax.random.split(jax.random.fold_in(key, 37), 3)
    first_draw = jax.random.randint(key_a, (device_total,), 1, PB_CAP + 1)
    second_draw = jax.random.randint(key_b, (device_total,), 1, PB_CAP + 1)
    live_slots = jnp.minimum(first_draw, second_draw)
    busiest = jax.random.randint(key_top, (), 0, device_total)
    live_slots = jnp.where(jnp.arange(device_total, dtype=jnp.int32) == busiest, PB_CAP, live_slots)
    return live_slots.astype(jnp.int32)


def draw_background(key, part):
    inner_key = jax.random.fold_in(key, 51)
    return jnp.clip(0.02 * jax.random.normal(inner_key, (G, G, G), jnp.float32), -0.12, 0.12)


def set_ends(array, rng, least, top_value):
    longest = array.shape.index(max(array.shape))
    spots = []
    for shift in (0, 1):
        where = [jax.random.randint(jax.random.fold_in(rng, axis), (), 0, length) for axis, length in enumerate(array.shape)]
        where[longest] = (where[longest] + shift) % array.shape[longest]
        spots.append(tuple(where))
    return array.at[spots[0]].set(least).at[spots[1]].set(top_value)


def levels(stream_key, extent, cuts, least, largest):
    factor_of, own = 1.0, jax.random.fold_in(stream_key, 6)
    for axis_at, blocks in cuts:
        steps = jnp.exp(jax.random.uniform(jax.random.fold_in(own, axis_at), (blocks,), jnp.float32, least / len(cuts), largest / len(cuts)))
        factor_of = factor_of * jnp.repeat(steps, extent[axis_at] // blocks).reshape([-1 if axis == axis_at else 1 for axis in range(len(extent))])
    return factor_of


def cumulative_ranks(number_of, skew):
    portions = [(1 << 20) // math.isqrt(rank ** skew) + 1 for rank in range(1, number_of + 1)]
    width = 1 + sum(portions) // (1 << 30)
    return np.cumsum(np.array([max(1, weight // width) for weight in portions]))


def ranked(own_key, extent, number_of, skew):
    grid = cumulative_ranks(number_of, skew)
    pick = jax.random.randint(jax.random.fold_in(own_key, 1), extent, 0, int(grid[number_of - 1]))
    rank = jnp.searchsorted(jnp.asarray(grid, jnp.int32), pick, side="right")
    return jax.random.permutation(jax.random.fold_in(own_key, 2), number_of)[rank].astype(jnp.int32)


def scatter_about(rng, dims, scale, limit, kind=jnp.bfloat16):
    return jnp.clip(scale * jax.random.normal(rng, dims, jnp.float32), -limit, limit).astype(kind)


def setup_inputs(seed: int = 0) -> dict:
    splits = jax.random.split(jax.random.key(seed), 13)
    return {
        "cell_index": draw_cell_index(jax.random.fold_in(splits[12], 71), 0),
        "offsets": jnp.clip(jax.random.uniform(splits[1], (3, ATOMS), jnp.float32, -0.5, 0.5) * levels(splits[1], (3, ATOMS), ((1, 32),), -0.4, 0.0), -0.5, 0.5),
        "species": set_ends(ranked(splits[2], (ATOMS,), NSPEC, 2), jax.random.fold_in(splits[2], 3), 0, NSPEC - 1).astype(jnp.int32),
        "pair_blocks": draw_pair_blocks(jax.random.fold_in(splits[12], 71), 0),
        "counts": draw_counts(jax.random.fold_in(splits[12], 71), 0),
        "background": draw_background(jax.random.fold_in(splits[12], 71), 0),
        "species_embed": scatter_about(splits[6], (NSPEC, D), 1.0, 6.0, jnp.float32),
        "neighbour_embed": scatter_about(splits[7], (NSPEC, D), 1.0, 6.0, jnp.float32),
        "w_radial": scatter_about(splits[8], (NBASIS, D), NBASIS ** -0.5, 2.0, jnp.float32),
        "w_hidden": scatter_about(splits[9], (D, D), D ** -0.5, 0.375),
        "w_charge": scatter_about(splits[10], (D,), D ** -0.5, 0.375),
        "w_energy": scatter_about(splits[11], (D,), D ** -0.5, 0.375),
    }


CUTOFF = 6.0
EWALD = 1.0
HIGHEST = lax.Precision.HIGHEST

def spline_weights(frac):
    return ((0.5 - frac) * (0.5 - frac) * 0.5, 0.75 - frac * frac, (0.5 + frac) * (0.5 + frac) * 0.5)

def spline_slopes(frac):
    return (frac - 0.5, -2.0 * frac, 0.5 + frac)

def green_table(freq_x, freq_y, freq_z):

    def signed(frequency):
        return jnp.where(frequency < G // 2, frequency, frequency - G)
    signed_x = signed(freq_x)
    signed_y = signed(freq_y)
    signed_z = signed(freq_z)
    squares = signed_x * signed_x + signed_y * signed_y + signed_z * signed_z
    wave_sq = squares.astype(jnp.float32) * (2.0 * math.pi / G * (2.0 * math.pi / G))
    safe_sq = jnp.where(squares > 0, wave_sq, 1.0)
    return jnp.where(squares > 0, 4.0 * math.pi * jnp.exp(-wave_sq / (4.0 * EWALD * EWALD)) / safe_sq, 0.0)

def pair_terms(pos_i, pos_j, embed_i, embed_j, self_mask, w_radial, w_hidden, w_charge, w_energy):
    separation = pos_j[:, None, :] - pos_i[:, :, None]
    half_box = 0.5 * G
    separation = jnp.where(separation > half_box, separation - G, jnp.where(separation < -half_box, separation + G, separation))
    distance = jnp.sqrt(lax.optimization_barrier(jnp.sum(separation * separation, axis=0)))
    scaled = distance / CUTOFF
    inside = 1.0 - scaled * scaled
    envelope = jnp.where(scaled < 1.0, inside * inside, 0.0)
    envelope = jnp.where(self_mask, 0.0, envelope)
    orders = jnp.arange(1, NBASIS + 1).astype(jnp.float32)
    radial = jnp.sinc(scaled[:, :, None] * orders)
    hidden_pre = jnp.einsum('ijn,nd->ijd', radial, w_radial, precision=HIGHEST) + embed_i[:, None, :] + embed_j[None, :, :]
    edge_feat = jax.nn.silu(hidden_pre).astype(jnp.bfloat16).reshape(-1, w_radial.shape[1])
    charge_pair = jnp.dot(edge_feat, w_charge, preferred_element_type=jnp.float32).reshape(envelope.shape)
    latent = jax.nn.silu(jnp.dot(edge_feat, w_hidden, preferred_element_type=jnp.float32)).astype(jnp.bfloat16)
    energy_pair = jnp.dot(latent, w_energy, preferred_element_type=jnp.float32).reshape(envelope.shape)
    return (lax.optimization_barrier(jnp.sum(envelope * energy_pair, axis=1)), lax.optimization_barrier(jnp.sum(envelope * charge_pair, axis=1)))

def reference(cell_index, offsets, species, pair_blocks, counts, background, species_embed, neighbour_embed, w_radial, w_hidden, w_charge, w_energy):
    positions = cell_index.astype(jnp.float32) + offsets
    device_count = N_GRP * N_DOM
    block_count = A_DEV // BLOCK

    def one_device(device):
        group_id = device // N_DOM
        domain_id = device % N_DOM
        left_dev = group_id * N_DOM + (domain_id + N_DOM - 1) % N_DOM
        right_dev = group_id * N_DOM + (domain_id + 1) % N_DOM

        def slice_pos(owner):
            return lax.dynamic_slice_in_dim(positions, (owner * A_DEV).astype(jnp.int32), A_DEV, 1)

        def slice_spec(owner):
            return lax.dynamic_slice_in_dim(species, (owner * A_DEV).astype(jnp.int32), A_DEV, 0)
        own_pos = slice_pos(device)
        ext_pos = jnp.concatenate([slice_pos(left_dev), own_pos, slice_pos(right_dev)], axis=1)
        own_embed = species_embed[slice_spec(device)]
        ext_embed = neighbour_embed[jnp.concatenate([slice_spec(left_dev), slice_spec(device), slice_spec(right_dev)], axis=0)]
        diagonal = jnp.arange(BLOCK, dtype=jnp.int32)[:, None] == jnp.arange(BLOCK, dtype=jnp.int32)[None, :]

        def visit_slot(slot_num, running):
            energy_acc, charge_acc = running
            row_id = (device * PB_CAP + slot_num).astype(jnp.int32)
            block_i = pair_blocks[row_id, 0]
            block_j = pair_blocks[row_id, 1]
            start_i = (block_i * BLOCK).astype(jnp.int32)
            start_j = (block_j * BLOCK).astype(jnp.int32)
            pos_i = lax.dynamic_slice_in_dim(own_pos, start_i, BLOCK, 1)
            pos_j = lax.dynamic_slice_in_dim(ext_pos, start_j, BLOCK, 1)
            embed_i = lax.dynamic_slice_in_dim(own_embed, start_i, BLOCK, 0)
            embed_j = lax.dynamic_slice_in_dim(ext_embed, start_j, BLOCK, 0)
            self_mask = (block_j == block_count + block_i) & diagonal
            energy_blk, charge_blk = pair_terms(pos_i, pos_j, embed_i, embed_j, self_mask, w_radial, w_hidden, w_charge, w_energy)
            energy_acc = lax.dynamic_update_slice_in_dim(energy_acc, lax.dynamic_slice_in_dim(energy_acc, start_i, BLOCK, 0) + energy_blk, start_i, 0)
            charge_acc = lax.dynamic_update_slice_in_dim(charge_acc, lax.dynamic_slice_in_dim(charge_acc, start_i, BLOCK, 0) + charge_blk, start_i, 0)
            return (energy_acc, charge_acc)
        blank_row = jnp.zeros((A_DEV,), jnp.float32)
        return lax.fori_loop(jnp.int32(0), counts[device], visit_slot, (blank_row, blank_row))
    energies, charges = lax.map(one_device, jnp.arange(device_count, dtype=jnp.int32))
    energies = energies.reshape(-1)
    charges = charges.reshape(-1)
    weights_x = spline_weights(offsets[0])
    weights_y = spline_weights(offsets[1])
    weights_z = spline_weights(offsets[2])
    slopes_x = spline_slopes(offsets[0])
    slopes_y = spline_slopes(offsets[1])
    slopes_z = spline_slopes(offsets[2])
    index_lists = []
    value_lists = []
    for step_x in range(3):
        for step_y in range(3):
            for step_z in range(3):
                point_x = (cell_index[0] + (step_x - 1)) % G
                point_y = (cell_index[1] + (step_y - 1)) % G
                point_z = (cell_index[2] + (step_z - 1)) % G
                index_lists.append((point_x, point_y, point_z))
                value_lists.append(weights_x[step_x] * weights_y[step_y] * weights_z[step_z] * charges)
    all_x = jnp.concatenate([entry[0] for entry in index_lists])
    all_y = jnp.concatenate([entry[1] for entry in index_lists])
    all_z = jnp.concatenate([entry[2] for entry in index_lists])
    density = background.at[all_x, all_y, all_z].add(jnp.concatenate(value_lists))
    frequency = jnp.arange(G, dtype=jnp.int32)
    green_vals = green_table(frequency[:, None, None], frequency[None, :, None], frequency[None, None, :])
    potential_grid = jnp.real(jnp.fft.ifftn(jnp.fft.fftn(density) * green_vals)).astype(jnp.float32)
    potential = jnp.zeros_like(charges)
    grad_x = jnp.zeros_like(charges)
    grad_y = jnp.zeros_like(charges)
    grad_z = jnp.zeros_like(charges)
    counter = 0
    for step_x in range(3):
        for step_y in range(3):
            for step_z in range(3):
                point_x, point_y, point_z = index_lists[counter]
                counter = counter + 1
                sampled = potential_grid[point_x, point_y, point_z]
                potential = potential + weights_x[step_x] * weights_y[step_y] * weights_z[step_z] * sampled
                grad_x = grad_x + slopes_x[step_x] * weights_y[step_y] * weights_z[step_z] * sampled
                grad_y = grad_y + weights_x[step_x] * slopes_y[step_y] * weights_z[step_z] * sampled
                grad_z = grad_z + weights_x[step_x] * weights_y[step_y] * slopes_z[step_z] * sampled
    electric_field = -jnp.stack([grad_x, grad_y, grad_z], axis=0)
    site_energy = energies + 0.5 * charges * potential
    return (site_energy, electric_field, charges)
```

```python
import functools
import math

import jax
import jax.numpy as jnp
import ml_dtypes
import numpy as np
from jax import lax
from jax.experimental import pallas as pl
from jax.experimental.pallas import tpu as pltpu
from jax.sharding import PartitionSpec as P

G = 256
NBASIS = 8
NSPEC = 8
BLOCK = 128
TILES_Y = 4
CUTOFF = 6.0
EWALD = 1.0
VMEM_BYTES = 56 << 20

BF = jnp.bfloat16
F32 = jnp.float32


def np_split(table):
    table = np.asarray(table, np.float32)
    high = table.astype(ml_dtypes.bfloat16)
    low = (table - high.astype(np.float32)).astype(ml_dtypes.bfloat16)
    return high, low


def hartley(points):
    phase = (np.arange(G)[:, None] * np.asarray(points)[None, :]) % G
    angle = phase.astype(np.float64) * (2.0 * math.pi / G)
    return np.cos(angle) + np.sin(angle)


def split2(x):
    high = x.astype(BF)
    low = (x - high.astype(F32)).astype(BF)
    return high, low


def dot_nn(a, b):
    return lax.dot_general(a, b, (((1,), (0,)), ((), ())), preferred_element_type=F32)


def dot_nt(a, b):
    return lax.dot_general(a, b, (((1,), (1,)), ((), ())), preferred_element_type=F32)


def dot3(dot, a, b):
    return dot(a[0], b[0]) + (dot(a[0], b[1]) + dot(a[1], b[0]))


def rounded(x):
    return lax.reduce_precision(x, exponent_bits=8, mantissa_bits=7)


def split3_outer(x):
    one = rounded(x)
    two = rounded(x - one)
    return one, two, rounded(x - one - two)


def split3(x):
    one = x.astype(BF).astype(F32)
    two = (x - one).astype(BF).astype(F32)
    three = (x - one - two).astype(BF).astype(F32)
    return one, two, three


def pair_kernel(
    slots, live, cols, ext, wcat, whid, wq, we, energy, charge, env_s, feat_s, kind_s, pq_s, pe_s, *, step
):
    blocks = energy.shape[0]
    energy[...] = jnp.zeros_like(energy)
    charge[...] = jnp.zeros_like(charge)
    half = 0.5 * G
    row8 = lax.broadcasted_iota(jnp.int32, (NSPEC, BLOCK), 0).astype(F32)
    diag = lax.broadcasted_iota(jnp.int32, (BLOCK, BLOCK), 0) == lax.broadcasted_iota(
        jnp.int32, (BLOCK, BLOCK), 1
    )

    def slot_body(slot, unused):
        bi = slots[slot, 0]
        bj = slots[slot, 1]
        ci = cols[pl.ds(pl.multiple_of(bi * BLOCK, BLOCK), BLOCK), :]
        rj = ext[:, pl.ds(pl.multiple_of(bj * BLOCK, BLOCK), BLOCK)]
        total = jnp.zeros((BLOCK, BLOCK), F32)
        for c in range(3):
            sep = rj[c : c + 1, :] - ci[:, c : c + 1]
            sep = jnp.where(sep > half, sep - G, jnp.where(sep < -half, sep + G, sep))
            total = total + sep * sep
        scaled = jnp.sqrt(total) / CUTOFF
        inside = 1.0 - scaled * scaled
        env = jnp.where(scaled < 1.0, inside * inside, 0.0)
        env = jnp.where(diag & (bj == blocks + bi), 0.0, env)
        env_s[...] = env
        kind_s[...] = jnp.broadcast_to(ci[:, 3:4], (BLOCK, BLOCK))
        theta = math.pi * jnp.minimum(scaled, 1.0)
        small = theta == 0.0
        inv = 1.0 / jnp.where(small, 1.0, theta)
        twice = 2.0 * jnp.cos(theta)
        before = jnp.zeros_like(theta)
        now = jnp.sin(theta)
        for n in range(1, NBASIS + 1):
            feat_s[pl.ds(n - 1, BLOCK, stride=NBASIS), :] = jnp.where(
                small, 1.0, now * inv * (1.0 / n)
            )
            before, now = now, twice * now - before
        kind_j = (row8 == rj[3:4, :]).astype(F32)

        def rows_body(it, unused_rows):
            i0 = it * step
            parts = []
            for k in range(step):
                i = i0 + k
                rad = feat_s[pl.ds(pl.multiple_of(i * NBASIS, NBASIS), NBASIS), :]
                one, two, three = split3(rad)
                kind_i = (row8 == kind_s[pl.ds(i, 1), :]).astype(F32)
                parts.append(
                    jnp.concatenate(
                        [one, one, one, two, two, three, kind_j, kind_j, kind_j, kind_i, kind_i, kind_i],
                        axis=0,
                    ).astype(BF)
                )
            feats = jnp.concatenate(parts, axis=1)
            h = dot_nn(wcat[...], feats)
            edge = (h + h * jnp.tanh(h)).astype(BF)
            cp = dot_nn(wq[...], edge)
            g = dot_nn(whid[...], edge)
            latent = (g + g * jnp.tanh(g)).astype(BF)
            ep = dot_nn(we[...], latent)
            for k in range(step):
                row = pl.ds(i0 + k, 1)
                env_row = env_s[row, :]
                pq_s[row, :] = env_row * cp[0:1, k * BLOCK : (k + 1) * BLOCK]
                pe_s[row, :] = env_row * ep[0:1, k * BLOCK : (k + 1) * BLOCK]
            return unused_rows

        lax.fori_loop(0, BLOCK // step, rows_body, 0)
        where = pl.ds(bi, 1)
        charge[where, :] = charge[where, :] + jnp.sum(pq_s[...].T, axis=0, keepdims=True)
        energy[where, :] = energy[where, :] + jnp.sum(pe_s[...].T, axis=0, keepdims=True)
        return unused

    lax.fori_loop(0, live[0], slot_body, 0)


def spline_rows(rows, first, center, frac, wrap, slopes):
    index = lax.broadcasted_iota(jnp.int32, (rows, frac.shape[1]), 0) + first
    if slopes:
        values = (frac - 0.5, -2.0 * frac, 0.5 + frac)
    else:
        values = ((0.5 - frac) * (0.5 - frac) * 0.5, 0.75 - frac * frac, (0.5 + frac) * (0.5 + frac) * 0.5)
    out = jnp.zeros((rows, frac.shape[1]), F32)
    for o in range(3):
        target = center + (o - 1)
        if wrap:
            target = jnp.where(target < 0, target + G, jnp.where(target >= G, target - G, target))
        out = jnp.where(index == target, values[o], out)
    return out


def chunk_blocks(blocks):
    per_tile = blocks // TILES_Y
    return [
        (t, [t + TILES_Y * z for z in range(2 * pair, 2 * pair + 2)])
        for t in range(TILES_Y)
        for pair in range(per_tile // 2)
    ]


def lanes_of(ref, row, pair):
    return jnp.concatenate([ref[row : row + 1, b * BLOCK : (b + 1) * BLOCK] for b in pair], axis=1)


def rows_of(ref, pair):
    return jnp.concatenate([ref[b : b + 1, :] for b in pair], axis=1)


def spread_kernel(local, frac, charge, back, hz_hi, hz_lo, out, acc):
    planes, padded_y, unused_z = acc.shape
    slab, quarter = back.shape[0], back.shape[1]
    window = 24
    tile = quarter // TILES_Y
    groups = out.shape[0]
    acc[...] = jnp.zeros_like(acc)
    acc[1 : slab + 1, 1 : quarter + 1, :] = back[...]
    for t, pair in chunk_blocks(charge.shape[0]):
        wx = spline_rows(planes, 0, lanes_of(local, 0, pair), lanes_of(frac, 0, pair), False, False)
        wy = spline_rows(window, tile * t, lanes_of(local, 1, pair), lanes_of(frac, 1, pair), False, False)
        wz = spline_rows(G, 0, lanes_of(local, 2, pair), lanes_of(frac, 2, pair), True, False)
        wy = wy * rows_of(charge, pair)
        mix = jnp.concatenate([wx[x : x + 1, :] * wy for x in range(planes)], axis=0)
        part = dot3(dot_nt, split2(mix), split2(wz))
        acc[:, tile * t : tile * t + window, :] += part.reshape(planes, window, G)
    low_half = lax.broadcasted_iota(jnp.int32, (padded_y, BLOCK), 1) < BLOCK // 2
    table = (hz_hi[...], hz_lo[...])
    for q in range(planes // 2):
        two = split2(acc[2 * q : 2 * q + 2].reshape(2 * padded_y, G))
        both = dot3(dot_nn, two, table)
        for s in range(groups):
            piece = both[:, s * BLOCK : (s + 1) * BLOCK]
            out[s, q] = jnp.where(low_half, piece[:padded_y], piece[padded_y:])


def y_kernel(data, hy_hi, hy_lo, out):
    groups, pairs = data.shape[0], data.shape[1]
    parts, rows = out.shape[0], out.shape[2]
    table = (hy_hi[...], hy_lo[...])
    for q in range(pairs):
        column = jnp.concatenate([data[g, q] for g in range(groups)], axis=0)
        result = dot3(dot_nn, table, split2(column))
        for d in range(parts):
            out[d, q] = result[d * rows : (d + 1) * rows]


def x_kernel(place, data, hx_hi, hx_lo, ix_hi, ix_lo, out, *, width_y):
    lines = data.shape[0] // width_y
    lane = lax.broadcasted_iota(jnp.int32, (lines, BLOCK), 1)
    low_half = lane < BLOCK // 2
    forward = (hx_hi[...], hx_lo[...])
    back = (ix_hi[...], ix_lo[...])
    grp_id = place[0]
    dom_id = place[1]

    def signed(m):
        return jnp.where(m < G // 2, m, m - G)

    shape = (G, BLOCK)
    mx = signed(lax.broadcasted_iota(jnp.int32, shape, 0))
    lanes = lax.broadcasted_iota(jnp.int32, shape, 1)
    in_high = lanes >= BLOCK // 2
    mz = signed(grp_id * (BLOCK // 2) + jnp.where(in_high, lanes - BLOCK // 2, lanes))
    base_sq = mx * mx + mz * mz
    unit = 2.0 * math.pi / G * (2.0 * math.pi / G)
    for pair in range(width_y // 2):
        first = pl.ds(2 * pair, lines, stride=width_y)
        second = pl.ds(2 * pair + 1, lines, stride=width_y)
        one = data[first, :]
        two = data[second, :]
        even = jnp.where(low_half, one, pltpu.roll(two, BLOCK // 2, 1))
        odd = jnp.where(low_half, pltpu.roll(one, BLOCK // 2, 1), two)
        column = jnp.concatenate([even, odd], axis=0)
        spectrum = dot3(dot_nn, forward, split2(column))
        my = signed(dom_id * width_y + 2 * pair + in_high.astype(jnp.int32))
        squares = base_sq + my * my
        wave = squares.astype(F32) * unit
        safe = jnp.where(squares > 0, wave, 1.0)
        green = jnp.where(
            squares > 0, 4.0 * math.pi * jnp.exp(-wave / (4.0 * EWALD * EWALD)) / safe, 0.0
        ) * (1.0 / (G * G * G))
        result = dot3(dot_nn, back, split2(spectrum * green))
        even = result[:lines]
        odd = result[lines:]
        out[first, :] = jnp.where(low_half, even, pltpu.roll(odd, BLOCK // 2, 1))
        out[second, :] = jnp.where(low_half, pltpu.roll(even, BLOCK // 2, 1), odd)


def sample_kernel(local, frac, charge, energy, data, hz_hi, hz_lo, site, field, mesh_s):
    planes, padded_y, unused_z = mesh_s.shape
    groups = data.shape[0]
    window = 24
    tile = (G // groups) // TILES_Y
    low_half = lax.broadcasted_iota(jnp.int32, (padded_y, BLOCK), 1) < BLOCK // 2
    table = (hz_hi[...], hz_lo[...])
    for q in range(planes // 2):
        evens = []
        odds = []
        for h in range(groups // 2):
            one = data[2 * h, q]
            two = data[2 * h + 1, q]
            evens.append(jnp.where(low_half, one, pltpu.roll(two, BLOCK // 2, 1)))
            odds.append(jnp.where(low_half, pltpu.roll(one, BLOCK // 2, 1), two))
        both = jnp.concatenate(
            [jnp.concatenate(evens, axis=1), jnp.concatenate(odds, axis=1)], axis=0
        )
        mesh_s[2 * q : 2 * q + 2] = dot3(dot_nn, split2(both), table).reshape(2, padded_y, G)
    for t, pair in chunk_blocks(charge.shape[0]):
        lx, fx = lanes_of(local, 0, pair), lanes_of(frac, 0, pair)
        ly, fy = lanes_of(local, 1, pair), lanes_of(frac, 1, pair)
        lz, fz = lanes_of(local, 2, pair), lanes_of(frac, 2, pair)
        wx = spline_rows(planes, 0, lx, fx, False, False)
        sx = spline_rows(planes, 0, lx, fx, False, True)
        wy = spline_rows(window, tile * t, ly, fy, False, False)
        sy = spline_rows(window, tile * t, ly, fy, False, True)
        wz = spline_rows(G, 0, lz, fz, True, False)
        sz = spline_rows(G, 0, lz, fz, True, True)
        strip = split2(mesh_s[:, tile * t : tile * t + window, :].reshape(planes * window, G))
        along = dot3(dot_nn, strip, split2(wz))
        slope = dot3(dot_nn, strip, split2(sz))
        value_y = jnp.zeros_like(wy)
        grad_y = jnp.zeros_like(wy)
        slope_y = jnp.zeros_like(wy)
        for x in range(planes):
            here = along[x * window : (x + 1) * window]
            value_y = value_y + wx[x : x + 1] * here
            grad_y = grad_y + sx[x : x + 1] * here
            slope_y = slope_y + wx[x : x + 1] * slope[x * window : (x + 1) * window]
        pot = jnp.sum(wy * value_y, axis=0, keepdims=True)
        rows = [
            -jnp.sum(wy * grad_y, axis=0, keepdims=True),
            -jnp.sum(sy * value_y, axis=0, keepdims=True),
            -jnp.sum(wy * slope_y, axis=0, keepdims=True),
        ]
        result = rows_of(energy, pair) + 0.5 * rows_of(charge, pair) * pot
        for k, b in enumerate(pair):
            cut = slice(k * BLOCK, (k + 1) * BLOCK)
            site[b : b + 1, :] = result[:, cut]
            for c in range(3):
                field[c : c + 1, b * BLOCK : (b + 1) * BLOCK] = rows[c][:, cut]


VMEM_SPEC = pl.BlockSpec(memory_space=pltpu.VMEM)
SMEM_SPEC = pl.BlockSpec(memory_space=pltpu.SMEM)


def call(body, outs, scratch, scalars, args):
    specs = [SMEM_SPEC] * scalars + [VMEM_SPEC] * (len(args) - scalars)
    many = isinstance(outs, (list, tuple))
    return pl.pallas_call(
        body,
        out_shape=outs,
        in_specs=specs,
        out_specs=[VMEM_SPEC] * len(outs) if many else VMEM_SPEC,
        scratch_shapes=scratch,
        compiler_params=pltpu.CompilerParams(vmem_limit_bytes=VMEM_BYTES),
    )(*args)


def pair_weights(species_embed, neighbour_embed, w_radial, w_hidden, w_charge, w_energy):
    r1, r2, r3 = split3_outer(w_radial)
    table = jnp.concatenate(
        [r1, r2, r3, r1, r2, r1, *split3_outer(neighbour_embed), *split3_outer(species_embed)], axis=0
    )
    wcat = (0.5 * table).T.astype(BF)
    whid = (0.5 * w_hidden.astype(F32)).T.astype(BF)
    width = w_charge.shape[0]
    wq = jnp.broadcast_to(w_charge[None, :], (16, width))
    we = jnp.broadcast_to(w_energy[None, :], (16, width))
    return wcat, whid, wq, we


def pair_call(pair_blocks, counts, record, extended, weights, blocks):
    cols = jnp.pad(record.T, ((0, 0), (0, 4)))
    shape = jax.ShapeDtypeStruct((blocks, BLOCK), F32)
    square = pltpu.VMEM((BLOCK, BLOCK), F32)
    return call(
        functools.partial(pair_kernel, step=4),
        [shape, shape],
        [square, pltpu.VMEM((BLOCK * NBASIS, BLOCK), F32), square, square, square],
        2,
        (pair_blocks, counts, cols, extended, *weights),
    )


def tables(slab, quarter, doms, groups, padded_y):
    planes = slab + 2
    points = np.arange(G)
    plain = hartley(points)
    half = G // groups
    order = np.concatenate([np.tile(np.arange(s * half, (s + 1) * half), 2) for s in range(groups)])
    hz_dup = plain[order].T
    hz_inv = plain
    y_points = np.array([quarter * g - 1 + r for g in range(groups) for r in range(padded_y)]) % G
    y_used = np.array([r < quarter + 2 for g in range(groups) for r in range(padded_y)])
    hy = hartley(y_points) * y_used[None, :]
    x_points = np.array(
        [slab * d - 1 + 2 * q + par for par in range(2) for d in range(doms) for q in range(planes // 2)]
    ) % G
    hx = hartley(x_points)
    return [np_split(t) for t in (hz_dup, hz_inv, hy, hy.T, hx, hx.T)]


def on_device(
    cell_index,
    offsets,
    species,
    pair_blocks,
    counts,
    background,
    species_embed,
    neighbour_embed,
    w_radial,
    w_hidden,
    w_charge,
    w_energy,
):
    atoms = cell_index.shape[1]
    blocks = atoms // BLOCK
    doms = lax.axis_size("dom")
    groups = lax.axis_size("grp")
    slab = G // doms
    quarter = G // groups
    planes = slab + 2
    pairs = planes // 2
    padded_y = quarter + 8
    width_y = G // doms
    dom_id = lax.axis_index("dom")
    grp_id = lax.axis_index("grp")
    hz_dup, hz_inv, hy, hy_inv, hx, hx_inv = tables(slab, quarter, doms, groups, padded_y)

    positions = cell_index.astype(F32) + offsets
    record = jnp.concatenate([positions, species.astype(F32)[None, :]], axis=0)
    left = lax.ppermute(record, "dom", [(i, (i + 1) % doms) for i in range(doms)])
    right = lax.ppermute(record, "dom", [((i + 1) % doms, i) for i in range(doms)])
    extended = jnp.concatenate([left, record, right], axis=1)
    weights = pair_weights(species_embed, neighbour_embed, w_radial, w_hidden, w_charge, w_energy)
    energies, charges = pair_call(pair_blocks, counts, record, extended, weights, blocks)

    origin = jnp.stack([1 - slab * dom_id, 1 - quarter * grp_id, jnp.zeros_like(dom_id)])
    local = cell_index + origin[:, None]
    spec = call(
        spread_kernel,
        jax.ShapeDtypeStruct((groups, pairs, padded_y, BLOCK), F32),
        [pltpu.VMEM((planes, padded_y, G), F32)],
        0,
        (local, offsets, charges, background, *hz_dup),
    )
    spec = lax.all_to_all(spec, "grp", 0, 0, tiled=True)
    spec = call(
        y_kernel, jax.ShapeDtypeStruct((doms, pairs, width_y, BLOCK), F32), [], 0, (spec, *hy)
    )
    spec = lax.all_to_all(spec, "dom", 0, 0, tiled=True)
    place = jnp.stack([grp_id, dom_id]).astype(jnp.int32)
    spec = call(
        functools.partial(x_kernel, width_y=width_y),
        jax.ShapeDtypeStruct((doms * pairs * width_y, BLOCK), F32),
        [],
        1,
        (place, spec.reshape(doms * pairs * width_y, BLOCK), *hx, *hx_inv),
    )
    spec = lax.all_to_all(spec.reshape(doms, pairs, width_y, BLOCK), "dom", 0, 0, tiled=True)
    spec = call(
        y_kernel, jax.ShapeDtypeStruct((groups, pairs, padded_y, BLOCK), F32), [], 0, (spec, *hy_inv)
    )
    spec = lax.all_to_all(spec, "grp", 0, 0, tiled=True)
    site, field = call(
        sample_kernel,
        [jax.ShapeDtypeStruct((blocks, BLOCK), F32), jax.ShapeDtypeStruct((3, atoms), F32)],
        [pltpu.VMEM((planes, padded_y, G), F32)],
        0,
        (local, offsets, charges, energies, spec, *hz_inv),
    )
    return (site.reshape(atoms), field, charges.reshape(atoms))


def solution(mesh):
    return jax.shard_map(
        on_device,
        mesh=mesh,
        in_specs=(
            P(None, ("grp", "dom")),
            P(None, ("grp", "dom")),
            P(("grp", "dom")),
            P(("grp", "dom"), None),
            P(("grp", "dom")),
            P("dom", "grp", None),
            P(),
            P(),
            P(),
            P(),
            P(),
            P(),
        ),
        out_specs=(P(("grp", "dom")), P(None, ("grp", "dom")), P(("grp", "dom"))),
        check_vma=False,
    )
```

```python
import functools
import math

import jax
import jax.numpy as jnp
import ml_dtypes
import numpy as np
from jax import lax
from jax.experimental import pallas as pl
from jax.experimental.pallas import tpu as pltpu
from jax.sharding import PartitionSpec as P

G = 256
NBASIS = 8
NSPEC = 8
BLOCK = 128
TILES_Y = 4
CUTOFF = 6.0
EWALD = 1.0
VMEM_BYTES = 56 << 20

BF = jnp.bfloat16
F32 = jnp.float32


def np_split(table):
    table = np.asarray(table, np.float32)
    high = table.astype(ml_dtypes.bfloat16)
    low = (table - high.astype(np.float32)).astype(ml_dtypes.bfloat16)
    return high, low


def hartley(points):
    phase = (np.arange(G)[:, None] * np.asarray(points)[None, :]) % G
    angle = phase.astype(np.float64) * (2.0 * math.pi / G)
    return np.cos(angle) + np.sin(angle)


def split2(x):
    high = x.astype(BF)
    low = (x - high.astype(F32)).astype(BF)
    return high, low


def dot_nn(a, b):
    return lax.dot_general(a, b, (((1,), (0,)), ((), ())), preferred_element_type=F32)


def dot_nt(a, b):
    return lax.dot_general(a, b, (((1,), (1,)), ((), ())), preferred_element_type=F32)


def dot3(dot, a, b):
    return dot(a[0], b[0]) + (dot(a[0], b[1]) + dot(a[1], b[0]))


def split3(x):
    one = x.astype(BF).astype(F32)
    two = (x - one).astype(BF).astype(F32)
    three = (x - one - two).astype(BF).astype(F32)
    return one, two, three


def pair_kernel(
    slots,
    live,
    left,
    own,
    right,
    radial_w,
    kind_i_w,
    kind_j_w,
    hidden_w,
    charge_w,
    energy_w,
    energy,
    charge,
    ext,
    wcat,
    whid,
    rank_s,
    theta_s,
    env_s,
    kind_s,
    *,
    step,
):
    blocks = energy.shape[0]
    atoms = own.shape[1]
    energy[...] = jnp.zeros_like(energy)
    charge[...] = jnp.zeros_like(charge)
    ext[:, :atoms] = left[...]
    ext[:, atoms : 2 * atoms] = own[...]
    ext[:, 2 * atoms :] = right[...]
    width = hidden_w.shape[0]
    r1, r2, r3 = split3(radial_w[...])
    table = jnp.concatenate(
        [
            *(r1, r2, r3, r1, r2, r1),
            *split3(kind_j_w[...]),
            *split3(kind_i_w[...]),
            jnp.zeros((BLOCK - 12 * NBASIS, width), F32),
        ],
        axis=0,
    )
    wcat[...] = (0.5 * table).T.astype(BF)
    whid[...] = (0.5 * hidden_w[...].astype(F32)).T.astype(BF)
    wq = jnp.broadcast_to(charge_w[...].astype(F32), (16, width)).astype(BF)
    we = jnp.broadcast_to(energy_w[...].astype(F32), (16, width)).astype(BF)
    half = 0.5 * G
    row8 = lax.broadcasted_iota(jnp.int32, (NSPEC, BLOCK), 0).astype(F32)
    sub = lax.broadcasted_iota(jnp.int32, (BLOCK, BLOCK), 0)
    lane = lax.broadcasted_iota(jnp.int32, (BLOCK, BLOCK), 1)
    earlier = (lane < sub).astype(F32).astype(BF)
    spare = jnp.zeros((BLOCK - 12 * NBASIS, BLOCK), F32)

    def slot_body(slot, unused):
        bi = slots[slot, 0]
        bj = slots[slot, 1]
        ri = own[:, pl.ds(pl.multiple_of(bi * BLOCK, BLOCK), BLOCK)]
        rj = ext[:, pl.ds(pl.multiple_of(bj * BLOCK, BLOCK), BLOCK)]
        total = jnp.zeros((BLOCK, BLOCK), F32)
        for c in range(3):
            sep = jnp.broadcast_to(rj[c : c + 1, :], (BLOCK, BLOCK)).T - ri[c : c + 1, :]
            sep = jnp.where(sep > half, sep - G, jnp.where(sep < -half, sep + G, sep))
            total = total + sep * sep
        scaled = jnp.sqrt(total) / CUTOFF
        inside = 1.0 - scaled * scaled
        env = jnp.where(scaled < 1.0, inside * inside, 0.0)
        env = jnp.where((sub == lane) & (bj == blocks + bi), 0.0, env)
        used = (env > 0.0).astype(F32)
        rank_s[...] = jnp.where(env > 0.0, dot_nn(earlier, used.astype(BF)), -1.0)
        theta_s[...] = math.pi * jnp.minimum(scaled, 1.0)
        env_s[...] = env
        kind_s[...] = jnp.broadcast_to(rj[3:4, :], (BLOCK, BLOCK)).T
        most = jnp.max(jnp.sum(used, axis=0, keepdims=True)).astype(jnp.int32)
        kind_i = (row8 == ri[3:4, :]).astype(F32)

        def rows_body(it, sums):
            energy_sum, charge_sum = sums
            rank = rank_s[...]
            parts = []
            envs = []
            for k in range(step):
                pick = rank == (it * step + k).astype(F32)
                theta = jnp.sum(jnp.where(pick, theta_s[...], 0.0), axis=0, keepdims=True)
                kind = jnp.sum(jnp.where(pick, kind_s[...], 0.0), axis=0, keepdims=True)
                envs.append(jnp.sum(jnp.where(pick, env_s[...], 0.0), axis=0, keepdims=True))
                phase = theta * (row8 + 1.0)
                small = phase == 0.0
                rad = jnp.where(small, 1.0, jnp.sin(phase) / jnp.where(small, 1.0, phase))
                one, two, three = split3(rad)
                kind_j = (row8 == kind).astype(F32)
                parts.append(
                    jnp.concatenate(
                        [
                            *(one, one, one, two, two, three),
                            *(kind_j, kind_j, kind_j, kind_i, kind_i, kind_i),
                            spare,
                        ],
                        axis=0,
                    ).astype(BF)
                )
            feats = jnp.concatenate(parts, axis=1)
            h = dot_nn(wcat[...], feats)
            edge = (h + h * jnp.tanh(h)).astype(BF)
            cp = dot_nn(wq, edge)
            g = dot_nn(whid[...], edge)
            latent = (g + g * jnp.tanh(g)).astype(BF)
            ep = dot_nn(we, latent)
            for k in range(step):
                cut = slice(k * BLOCK, (k + 1) * BLOCK)
                charge_sum = charge_sum + envs[k] * cp[0:1, cut]
                energy_sum = energy_sum + envs[k] * ep[0:1, cut]
            return energy_sum, charge_sum

        zero = jnp.zeros((1, BLOCK), F32)
        energy_sum, charge_sum = lax.fori_loop(
            0, (most + step - 1) // step, rows_body, (zero, zero)
        )
        where = pl.ds(bi, 1)
        charge[where, :] = charge[where, :] + charge_sum
        energy[where, :] = energy[where, :] + energy_sum
        return unused

    lax.fori_loop(0, live[0], slot_body, 0)


def spline_rows(rows, first, center, frac, wrap, slopes):
    index = lax.broadcasted_iota(jnp.int32, (rows, frac.shape[1]), 0) + first
    if slopes:
        values = (frac - 0.5, -2.0 * frac, 0.5 + frac)
    else:
        values = ((0.5 - frac) * (0.5 - frac) * 0.5, 0.75 - frac * frac, (0.5 + frac) * (0.5 + frac) * 0.5)
    out = jnp.zeros((rows, frac.shape[1]), F32)
    for o in range(3):
        target = center + (o - 1)
        if wrap:
            target = jnp.where(target < 0, target + G, jnp.where(target >= G, target - G, target))
        out = jnp.where(index == target, values[o], out)
    return out


def chunk_blocks(blocks):
    per_tile = blocks // TILES_Y
    return [
        (t, [t + TILES_Y * z for z in range(2 * pair, 2 * pair + 2)])
        for t in range(TILES_Y)
        for pair in range(per_tile // 2)
    ]


def lanes_of(ref, row, pair):
    return jnp.concatenate([ref[row : row + 1, b * BLOCK : (b + 1) * BLOCK] for b in pair], axis=1)


def rows_of(ref, pair):
    return jnp.concatenate([ref[b : b + 1, :] for b in pair], axis=1)


def spread_kernel(local, frac, charge, back, hz_hi, hz_lo, out, acc):
    planes, padded_y, unused_z = acc.shape
    slab, quarter = back.shape[0], back.shape[1]
    window = 24
    tile = quarter // TILES_Y
    groups = out.shape[0]
    acc[...] = jnp.zeros_like(acc)
    acc[1 : slab + 1, 1 : quarter + 1, :] = back[...]
    for t, pair in chunk_blocks(charge.shape[0]):
        wx = spline_rows(planes, 0, lanes_of(local, 0, pair), lanes_of(frac, 0, pair), False, False)
        wy = spline_rows(window, tile * t, lanes_of(local, 1, pair), lanes_of(frac, 1, pair), False, False)
        wz = spline_rows(G, 0, lanes_of(local, 2, pair), lanes_of(frac, 2, pair), True, False)
        wy = wy * rows_of(charge, pair)
        mix = jnp.concatenate([wx[x : x + 1, :] * wy for x in range(planes)], axis=0)
        part = dot3(dot_nt, split2(mix), split2(wz))
        acc[:, tile * t : tile * t + window, :] += part.reshape(planes, window, G)
    low_half = lax.broadcasted_iota(jnp.int32, (padded_y, BLOCK), 1) < BLOCK // 2
    table = (hz_hi[...], hz_lo[...])
    for q in range(planes // 2):
        two = split2(acc[2 * q : 2 * q + 2].reshape(2 * padded_y, G))
        both = dot3(dot_nn, two, table)
        for s in range(groups):
            piece = both[:, s * BLOCK : (s + 1) * BLOCK]
            out[s, q] = jnp.where(low_half, piece[:padded_y], piece[padded_y:])


def y_kernel(data, hy_hi, hy_lo, out):
    groups, pairs = data.shape[0], data.shape[1]
    parts, rows = out.shape[0], out.shape[2]
    table = (hy_hi[...], hy_lo[...])
    for q in range(pairs):
        column = jnp.concatenate([data[g, q] for g in range(groups)], axis=0)
        result = dot3(dot_nn, table, split2(column))
        for d in range(parts):
            out[d, q] = result[d * rows : (d + 1) * rows]


def x_kernel(place, data, hx_hi, hx_lo, ix_hi, ix_lo, out, *, width_y):
    lines = data.shape[0] // width_y
    lane = lax.broadcasted_iota(jnp.int32, (lines, BLOCK), 1)
    low_half = lane < BLOCK // 2
    forward = (hx_hi[...], hx_lo[...])
    back = (ix_hi[...], ix_lo[...])
    grp_id = place[0]
    dom_id = place[1]

    def signed(m):
        return jnp.where(m < G // 2, m, m - G)

    shape = (G, BLOCK)
    mx = signed(lax.broadcasted_iota(jnp.int32, shape, 0))
    lanes = lax.broadcasted_iota(jnp.int32, shape, 1)
    in_high = lanes >= BLOCK // 2
    mz = signed(grp_id * (BLOCK // 2) + jnp.where(in_high, lanes - BLOCK // 2, lanes))
    base_sq = mx * mx + mz * mz
    unit = 2.0 * math.pi / G * (2.0 * math.pi / G)
    for pair in range(width_y // 2):
        first = pl.ds(2 * pair, lines, stride=width_y)
        second = pl.ds(2 * pair + 1, lines, stride=width_y)
        one = data[first, :]
        two = data[second, :]
        even = jnp.where(low_half, one, pltpu.roll(two, BLOCK // 2, 1))
        odd = jnp.where(low_half, pltpu.roll(one, BLOCK // 2, 1), two)
        column = jnp.concatenate([even, odd], axis=0)
        spectrum = dot3(dot_nn, forward, split2(column))
        my = signed(dom_id * width_y + 2 * pair + in_high.astype(jnp.int32))
        squares = base_sq + my * my
        wave = squares.astype(F32) * unit
        safe = jnp.where(squares > 0, wave, 1.0)
        green = jnp.where(
            squares > 0, 4.0 * math.pi * jnp.exp(-wave / (4.0 * EWALD * EWALD)) / safe, 0.0
        ) * (1.0 / (G * G * G))
        result = dot3(dot_nn, back, split2(spectrum * green))
        even = result[:lines]
        odd = result[lines:]
        out[first, :] = jnp.where(low_half, even, pltpu.roll(odd, BLOCK // 2, 1))
        out[second, :] = jnp.where(low_half, pltpu.roll(even, BLOCK // 2, 1), odd)


def sample_kernel(local, frac, charge, energy, data, hz_hi, hz_lo, site, field, mesh_s):
    planes, padded_y, unused_z = mesh_s.shape
    groups = data.shape[0]
    window = 24
    tile = (G // groups) // TILES_Y
    low_half = lax.broadcasted_iota(jnp.int32, (padded_y, BLOCK), 1) < BLOCK // 2
    table = (hz_hi[...], hz_lo[...])
    for q in range(planes // 2):
        evens = []
        odds = []
        for h in range(groups // 2):
            one = data[2 * h, q]
            two = data[2 * h + 1, q]
            evens.append(jnp.where(low_half, one, pltpu.roll(two, BLOCK // 2, 1)))
            odds.append(jnp.where(low_half, pltpu.roll(one, BLOCK // 2, 1), two))
        both = jnp.concatenate(
            [jnp.concatenate(evens, axis=1), jnp.concatenate(odds, axis=1)], axis=0
        )
        mesh_s[2 * q : 2 * q + 2] = dot3(dot_nn, split2(both), table).reshape(2, padded_y, G)
    for t, pair in chunk_blocks(charge.shape[0]):
        lx, fx = lanes_of(local, 0, pair), lanes_of(frac, 0, pair)
        ly, fy = lanes_of(local, 1, pair), lanes_of(frac, 1, pair)
        lz, fz = lanes_of(local, 2, pair), lanes_of(frac, 2, pair)
        wx = spline_rows(planes, 0, lx, fx, False, False)
        sx = spline_rows(planes, 0, lx, fx, False, True)
        wy = spline_rows(window, tile * t, ly, fy, False, False)
        sy = spline_rows(window, tile * t, ly, fy, False, True)
        wz = spline_rows(G, 0, lz, fz, True, False)
        sz = spline_rows(G, 0, lz, fz, True, True)
        strip = split2(mesh_s[:, tile * t : tile * t + window, :].reshape(planes * window, G))
        along = dot3(dot_nn, strip, split2(wz))
        slope = dot3(dot_nn, strip, split2(sz))
        value_y = jnp.zeros_like(wy)
        grad_y = jnp.zeros_like(wy)
        slope_y = jnp.zeros_like(wy)
        for x in range(planes):
            here = along[x * window : (x + 1) * window]
            value_y = value_y + wx[x : x + 1] * here
            grad_y = grad_y + sx[x : x + 1] * here
            slope_y = slope_y + wx[x : x + 1] * slope[x * window : (x + 1) * window]
        pot = jnp.sum(wy * value_y, axis=0, keepdims=True)
        rows = [
            -jnp.sum(wy * grad_y, axis=0, keepdims=True),
            -jnp.sum(sy * value_y, axis=0, keepdims=True),
            -jnp.sum(wy * slope_y, axis=0, keepdims=True),
        ]
        result = rows_of(energy, pair) + 0.5 * rows_of(charge, pair) * pot
        for k, b in enumerate(pair):
            cut = slice(k * BLOCK, (k + 1) * BLOCK)
            site[b : b + 1, :] = result[:, cut]
            for c in range(3):
                field[c : c + 1, b * BLOCK : (b + 1) * BLOCK] = rows[c][:, cut]


VMEM_SPEC = pl.BlockSpec(memory_space=pltpu.VMEM)
SMEM_SPEC = pl.BlockSpec(memory_space=pltpu.SMEM)


def call(body, outs, scratch, scalars, args):
    specs = [SMEM_SPEC] * scalars + [VMEM_SPEC] * (len(args) - scalars)
    many = isinstance(outs, (list, tuple))
    return pl.pallas_call(
        body,
        out_shape=outs,
        in_specs=specs,
        out_specs=[VMEM_SPEC] * len(outs) if many else VMEM_SPEC,
        scratch_shapes=scratch,
        compiler_params=pltpu.CompilerParams(vmem_limit_bytes=VMEM_BYTES),
    )(*args)


def pair_call(
    pair_blocks, counts, left, record, right, species_embed, neighbour_embed, w_radial, w_hidden, w_charge, w_energy
):
    blocks = record.shape[1] // BLOCK
    width = w_charge.shape[0]
    shape = jax.ShapeDtypeStruct((blocks, BLOCK), F32)
    square = pltpu.VMEM((BLOCK, BLOCK), F32)
    return call(
        functools.partial(pair_kernel, step=4),
        [shape, shape],
        [
            pltpu.VMEM((record.shape[0], 3 * record.shape[1]), F32),
            pltpu.VMEM((width, BLOCK), BF),
            pltpu.VMEM((width, width), BF),
            *[square] * 4,
        ],
        2,
        (
            pair_blocks,
            counts,
            left,
            record,
            right,
            w_radial,
            species_embed,
            neighbour_embed,
            w_hidden,
            w_charge[None, :],
            w_energy[None, :],
        ),
    )


def tables(slab, quarter, doms, groups, padded_y):
    planes = slab + 2
    points = np.arange(G)
    plain = hartley(points)
    half = G // groups
    order = np.concatenate([np.tile(np.arange(s * half, (s + 1) * half), 2) for s in range(groups)])
    hz_dup = plain[order].T
    hz_inv = plain
    y_points = np.array([quarter * g - 1 + r for g in range(groups) for r in range(padded_y)]) % G
    y_used = np.array([r < quarter + 2 for g in range(groups) for r in range(padded_y)])
    hy = hartley(y_points) * y_used[None, :]
    x_points = np.array(
        [slab * d - 1 + 2 * q + par for par in range(2) for d in range(doms) for q in range(planes // 2)]
    ) % G
    hx = hartley(x_points)
    return [np_split(t) for t in (hz_dup, hz_inv, hy, hy.T, hx, hx.T)]


def on_device(
    cell_index,
    offsets,
    species,
    pair_blocks,
    counts,
    background,
    species_embed,
    neighbour_embed,
    w_radial,
    w_hidden,
    w_charge,
    w_energy,
):
    atoms = cell_index.shape[1]
    blocks = atoms // BLOCK
    doms = lax.axis_size("dom")
    groups = lax.axis_size("grp")
    slab = G // doms
    quarter = G // groups
    planes = slab + 2
    pairs = planes // 2
    padded_y = quarter + 8
    width_y = G // doms
    dom_id = lax.axis_index("dom")
    grp_id = lax.axis_index("grp")
    hz_dup, hz_inv, hy, hy_inv, hx, hx_inv = tables(slab, quarter, doms, groups, padded_y)

    positions = cell_index.astype(F32) + offsets
    record = jnp.concatenate([positions, species.astype(F32)[None, :]], axis=0)
    left = lax.ppermute(record, "dom", [(i, (i + 1) % doms) for i in range(doms)])
    right = lax.ppermute(record, "dom", [((i + 1) % doms, i) for i in range(doms)])
    energies, charges = pair_call(
        pair_blocks,
        counts,
        left,
        record,
        right,
        species_embed,
        neighbour_embed,
        w_radial,
        w_hidden,
        w_charge,
        w_energy,
    )

    origin = jnp.stack([1 - slab * dom_id, 1 - quarter * grp_id, jnp.zeros_like(dom_id)])
    local = cell_index + origin[:, None]
    spec = call(
        spread_kernel,
        jax.ShapeDtypeStruct((groups, pairs, padded_y, BLOCK), F32),
        [pltpu.VMEM((planes, padded_y, G), F32)],
        0,
        (local, offsets, charges, background, *hz_dup),
    )
    spec = lax.all_to_all(spec, "grp", 0, 0, tiled=True)
    spec = call(
        y_kernel, jax.ShapeDtypeStruct((doms, pairs, width_y, BLOCK), F32), [], 0, (spec, *hy)
    )
    spec = lax.all_to_all(spec, "dom", 0, 0, tiled=True)
    place = jnp.stack([grp_id, dom_id]).astype(jnp.int32)
    spec = call(
        functools.partial(x_kernel, width_y=width_y),
        jax.ShapeDtypeStruct((doms * pairs * width_y, BLOCK), F32),
        [],
        1,
        (place, spec.reshape(doms * pairs * width_y, BLOCK), *hx, *hx_inv),
    )
    spec = lax.all_to_all(spec.reshape(doms, pairs, width_y, BLOCK), "dom", 0, 0, tiled=True)
    spec = call(
        y_kernel, jax.ShapeDtypeStruct((groups, pairs, padded_y, BLOCK), F32), [], 0, (spec, *hy_inv)
    )
    spec = lax.all_to_all(spec, "grp", 0, 0, tiled=True)
    site, field = call(
        sample_kernel,
        [jax.ShapeDtypeStruct((blocks, BLOCK), F32), jax.ShapeDtypeStruct((3, atoms), F32)],
        [pltpu.VMEM((planes, padded_y, G), F32)],
        0,
        (local, offsets, charges, energies, spec, *hz_inv),
    )
    return (site.reshape(atoms), field, charges.reshape(atoms))


def solution(mesh):
    return jax.shard_map(
        on_device,
        mesh=mesh,
        in_specs=(
            P(None, ("grp", "dom")),
            P(None, ("grp", "dom")),
            P(("grp", "dom")),
            P(("grp", "dom"), None),
            P(("grp", "dom")),
            P("dom", "grp", None),
            P(),
            P(),
            P(),
            P(),
            P(),
            P(),
        ),
        out_specs=(P(("grp", "dom")), P(None, ("grp", "dom")), P(("grp", "dom"))),
        check_vma=False,
    )
```

```python
import functools
import math

import jax
import jax.numpy as jnp
import ml_dtypes
import numpy as np
from jax import lax
from jax.experimental import pallas as pl
from jax.experimental.pallas import tpu as pltpu
from jax.sharding import PartitionSpec as P

G = 256
NBASIS = 8
NSPEC = 8
BLOCK = 128
TILES_Y = 4
CUTOFF = 6.0
EWALD = 1.0
VMEM_BYTES = 56 << 20

BF = jnp.bfloat16
F32 = jnp.float32


def np_split(table):
    table = np.asarray(table, np.float32)
    high = table.astype(ml_dtypes.bfloat16)
    low = (table - high.astype(np.float32)).astype(ml_dtypes.bfloat16)
    return high, low


def hartley(points):
    phase = (np.arange(G)[:, None] * np.asarray(points)[None, :]) % G
    angle = phase.astype(np.float64) * (2.0 * math.pi / G)
    return np.cos(angle) + np.sin(angle)


def split2(x):
    high = x.astype(BF)
    low = (x - high.astype(F32)).astype(BF)
    return high, low


def dot_nn(a, b):
    return lax.dot_general(a, b, (((1,), (0,)), ((), ())), preferred_element_type=F32)


def dot_nt(a, b):
    return lax.dot_general(a, b, (((1,), (1,)), ((), ())), preferred_element_type=F32)


def dot3(dot, a, b):
    return dot(a[0], b[0]) + (dot(a[0], b[1]) + dot(a[1], b[0]))


def split3(x):
    one = x.astype(BF).astype(F32)
    two = (x - one).astype(BF).astype(F32)
    three = (x - one - two).astype(BF).astype(F32)
    return one, two, three


def pair_kernel(
    slots,
    live,
    left,
    own,
    right,
    radial_w,
    kind_i_w,
    kind_j_w,
    hidden_w,
    charge_w,
    energy_w,
    energy,
    charge,
    ext,
    wcat,
    whid,
    rank_s,
    theta_s,
    env_s,
    kind_s,
    *,
    step,
):
    blocks = energy.shape[0]
    atoms = own.shape[1]
    energy[...] = jnp.zeros_like(energy)
    charge[...] = jnp.zeros_like(charge)
    ext[:, :atoms] = left[...]
    ext[:, atoms : 2 * atoms] = own[...]
    ext[:, 2 * atoms :] = right[...]
    width = hidden_w.shape[0]
    r1, r2, r3 = split3(radial_w[...])
    table = jnp.concatenate(
        [
            *(r1, r2, r3, r1, r2, r1),
            *split3(kind_j_w[...]),
            *split3(kind_i_w[...]),
            jnp.zeros((BLOCK - 12 * NBASIS, width), F32),
        ],
        axis=0,
    )
    wcat[...] = (0.5 * table).T.astype(BF)
    whid[...] = (0.5 * hidden_w[...].astype(F32)).T.astype(BF)
    wq = jnp.broadcast_to(charge_w[...].astype(F32), (16, width)).astype(BF)
    we = jnp.broadcast_to(energy_w[...].astype(F32), (16, width)).astype(BF)
    half = 0.5 * G
    row8 = lax.broadcasted_iota(jnp.int32, (NSPEC, BLOCK), 0).astype(F32)
    sub = lax.broadcasted_iota(jnp.int32, (BLOCK, BLOCK), 0)
    lane = lax.broadcasted_iota(jnp.int32, (BLOCK, BLOCK), 1)
    earlier = (lane < sub).astype(F32).astype(BF)
    spare = jnp.zeros((BLOCK - 12 * NBASIS, BLOCK), F32)

    def slot_body(slot, unused):
        bi = slots[slot, 0]
        bj = slots[slot, 1]
        ri = own[:, pl.ds(pl.multiple_of(bi * BLOCK, BLOCK), BLOCK)]
        rj = ext[:, pl.ds(pl.multiple_of(bj * BLOCK, BLOCK), BLOCK)]
        total = jnp.zeros((BLOCK, BLOCK), F32)
        for c in range(3):
            sep = jnp.broadcast_to(rj[c : c + 1, :], (BLOCK, BLOCK)).T - ri[c : c + 1, :]
            sep = jnp.where(sep > half, sep - G, jnp.where(sep < -half, sep + G, sep))
            total = total + sep * sep
        scaled = jnp.sqrt(total) / CUTOFF
        inside = 1.0 - scaled * scaled
        env = jnp.where(scaled < 1.0, inside * inside, 0.0)
        env = jnp.where((sub == lane) & (bj == blocks + bi), 0.0, env)
        used = (env > 0.0).astype(F32)
        rank_s[...] = jnp.where(env > 0.0, dot_nn(earlier, used.astype(BF)), -1.0)
        theta_s[...] = math.pi * jnp.minimum(scaled, 1.0)
        env_s[...] = env
        kind_s[...] = jnp.broadcast_to(rj[3:4, :], (BLOCK, BLOCK)).T
        most = jnp.max(jnp.sum(used, axis=0, keepdims=True)).astype(jnp.int32)
        kind_i = (row8 == ri[3:4, :]).astype(F32)

        def rows_body(it, sums):
            energy_sum, charge_sum = sums
            rank = rank_s[...]
            parts = []
            envs = []
            for k in range(step):
                pick = rank == (it * step + k).astype(F32)
                theta = jnp.sum(jnp.where(pick, theta_s[...], 0.0), axis=0, keepdims=True)
                kind = jnp.sum(jnp.where(pick, kind_s[...], 0.0), axis=0, keepdims=True)
                envs.append(jnp.sum(jnp.where(pick, env_s[...], 0.0), axis=0, keepdims=True))
                phase = theta * (row8 + 1.0)
                small = phase == 0.0
                rad = jnp.where(small, 1.0, jnp.sin(phase) / jnp.where(small, 1.0, phase))
                one, two, three = split3(rad)
                kind_j = (row8 == kind).astype(F32)
                parts.append(
                    jnp.concatenate(
                        [
                            *(one, one, one, two, two, three),
                            *(kind_j, kind_j, kind_j, kind_i, kind_i, kind_i),
                            spare,
                        ],
                        axis=0,
                    ).astype(BF)
                )
            feats = jnp.concatenate(parts, axis=1)
            h = dot_nn(wcat[...], feats)
            edge = (h + h * jnp.tanh(h)).astype(BF)
            cp = dot_nn(wq, edge)
            g = dot_nn(whid[...], edge)
            latent = (g + g * jnp.tanh(g)).astype(BF)
            ep = dot_nn(we, latent)
            for k in range(step):
                cut = slice(k * BLOCK, (k + 1) * BLOCK)
                charge_sum = charge_sum + envs[k] * cp[0:1, cut]
                energy_sum = energy_sum + envs[k] * ep[0:1, cut]
            return energy_sum, charge_sum

        zero = jnp.zeros((1, BLOCK), F32)
        energy_sum, charge_sum = lax.fori_loop(
            0, (most + step - 1) // step, rows_body, (zero, zero)
        )
        where = pl.ds(bi, 1)
        charge[where, :] = charge[where, :] + charge_sum
        energy[where, :] = energy[where, :] + energy_sum
        return unused

    lax.fori_loop(0, live[0], slot_body, 0)


def spline_rows(rows, first, center, frac, wrap, slopes):
    index = lax.broadcasted_iota(jnp.int32, (rows, frac.shape[1]), 0) + first
    if slopes:
        values = (frac - 0.5, -2.0 * frac, 0.5 + frac)
    else:
        values = ((0.5 - frac) * (0.5 - frac) * 0.5, 0.75 - frac * frac, (0.5 + frac) * (0.5 + frac) * 0.5)
    out = jnp.zeros((rows, frac.shape[1]), F32)
    for o in range(3):
        target = center + (o - 1)
        if wrap:
            target = jnp.where(target < 0, target + G, jnp.where(target >= G, target - G, target))
        out = jnp.where(index == target, values[o], out)
    return out


def chunk_blocks(blocks):
    per_tile = blocks // TILES_Y
    return [
        (t, [t + TILES_Y * z for z in range(2 * pair, 2 * pair + 2)])
        for t in range(TILES_Y)
        for pair in range(per_tile // 2)
    ]


def lanes_of(ref, row, pair):
    return jnp.concatenate([ref[row : row + 1, b * BLOCK : (b + 1) * BLOCK] for b in pair], axis=1)


def rows_of(ref, pair):
    return jnp.concatenate([ref[b : b + 1, :] for b in pair], axis=1)


def spread_kernel(local, frac, charge, back, hz_hi, hz_lo, out, acc):
    planes, padded_y, unused_z = acc.shape
    slab, quarter = back.shape[0], back.shape[1]
    window = 24
    tile = quarter // TILES_Y
    groups = out.shape[0]
    acc[...] = jnp.zeros_like(acc)
    acc[1 : slab + 1, 1 : quarter + 1, :] = back[...]
    for t, pair in chunk_blocks(charge.shape[0]):
        wx = spline_rows(planes, 0, lanes_of(local, 0, pair), lanes_of(frac, 0, pair), False, False)
        wy = spline_rows(window, tile * t, lanes_of(local, 1, pair), lanes_of(frac, 1, pair), False, False)
        wz = spline_rows(G, 0, lanes_of(local, 2, pair), lanes_of(frac, 2, pair), True, False)
        wy = wy * rows_of(charge, pair)
        mix = jnp.concatenate([wx[x : x + 1, :] * wy for x in range(planes)], axis=0)
        part = dot3(dot_nt, split2(mix), split2(wz))
        acc[:, tile * t : tile * t + window, :] += part.reshape(planes, window, G)
    low_half = lax.broadcasted_iota(jnp.int32, (padded_y, BLOCK), 1) < BLOCK // 2
    table = (hz_hi[...], hz_lo[...])
    for q in range(planes // 2):
        two = split2(acc[2 * q : 2 * q + 2].reshape(2 * padded_y, G))
        both = dot3(dot_nn, two, table)
        for s in range(groups):
            piece = both[:, s * BLOCK : (s + 1) * BLOCK]
            out[s, q] = jnp.where(low_half, piece[:padded_y], piece[padded_y:])


def hop_kernel(
    data, hy_hi, hy_lo, out, land, ready, send1, recv1, send2, recv2, local1, local2, *, axis1, axis2, cuts
):
    n1, n2 = land.shape[0], out.shape[0]
    rows = out.shape[2]
    me1, me2 = lax.axis_index(axis1), lax.axis_index(axis2)
    mesh_ids = pl.DeviceIdType.MESH
    barrier = pltpu.get_barrier_semaphore()
    for axis, me, count in ((axis1, me1, n1), (axis2, me2, n2)):
        for k in range(1, count):
            pl.semaphore_signal(
                barrier, inc=1, device_id={axis: lax.rem(me + k, count)}, device_id_type=mesh_ids
            )
    pl.semaphore_wait(barrier, n1 + n2 - 2)

    def send(src, dst, send_sem, recv_sem, axis, me, count, k, c, part):
        peer = lax.rem(me + k, count)
        copy = pltpu.make_async_remote_copy(
            src_ref=src.at[peer, part],
            dst_ref=dst.at[me, part],
            send_sem=send_sem.at[c, k - 1],
            recv_sem=recv_sem.at[c, k - 1],
            device_id={axis: peer},
            device_id_type=mesh_ids,
        )
        copy.start()
        return copy

    first = []
    for c, (lo, hi) in enumerate(cuts):
        part = pl.ds(lo, hi - lo)
        mine = pltpu.make_async_copy(data.at[me1, part], land.at[me1, part], local1.at[c])
        mine.start()
        first.append(
            (mine, [send(data, land, send1, recv1, axis1, me1, n1, k, c, part) for k in range(1, n1)])
        )
    table = (hy_hi[...], hy_lo[...])
    second = []
    for c, (lo, hi) in enumerate(cuts):
        part = pl.ds(lo, hi - lo)
        mine, copies = first[c]
        mine.wait()
        for copy in copies:
            copy.wait_recv()
        for q in range(lo, hi):
            column = jnp.concatenate([land[g, q] for g in range(n1)], axis=0)
            result = dot3(dot_nn, table, split2(column))
            for d in range(n2):
                ready[d, q] = result[d * rows : (d + 1) * rows]
        own = pltpu.make_async_copy(ready.at[me2, part], out.at[me2, part], local2.at[c])
        own.start()
        second.append(
            (own, [send(ready, out, send2, recv2, axis2, me2, n2, k, c, part) for k in range(1, n2)])
        )
    for mine, copies in first:
        for copy in copies:
            copy.wait_send()
    for own, copies in second:
        own.wait()
        for copy in copies:
            copy.wait()


def hop_call(data, table, out_shape, axis1, axis2, collective):
    n1, pairs = data.shape[0], data.shape[1]
    n2 = out_shape[0]
    chunks = min(4, pairs)
    ends = [round(pairs * c / chunks) for c in range(chunks + 1)]
    dma = pltpu.SemaphoreType.DMA
    return pl.pallas_call(
        functools.partial(hop_kernel, axis1=axis1, axis2=axis2, cuts=tuple(zip(ends[:-1], ends[1:]))),
        out_shape=jax.ShapeDtypeStruct(out_shape, F32),
        in_specs=[VMEM_SPEC] * 3,
        out_specs=VMEM_SPEC,
        scratch_shapes=[
            pltpu.VMEM(data.shape, F32),
            pltpu.VMEM(out_shape, F32),
            *[dma((chunks, n1 - 1))] * 2,
            *[dma((chunks, n2 - 1))] * 2,
            *[dma((chunks,))] * 2,
        ],
        compiler_params=pltpu.CompilerParams(
            vmem_limit_bytes=VMEM_BYTES, collective_id=collective, has_side_effects=True
        ),
    )(data, *table)


def x_kernel(place, data, hx_hi, hx_lo, ix_hi, ix_lo, out, *, width_y):
    lines = data.shape[0] // width_y
    lane = lax.broadcasted_iota(jnp.int32, (lines, BLOCK), 1)
    low_half = lane < BLOCK // 2
    forward = (hx_hi[...], hx_lo[...])
    back = (ix_hi[...], ix_lo[...])
    grp_id = place[0]
    dom_id = place[1]

    def signed(m):
        return jnp.where(m < G // 2, m, m - G)

    shape = (G, BLOCK)
    mx = signed(lax.broadcasted_iota(jnp.int32, shape, 0))
    lanes = lax.broadcasted_iota(jnp.int32, shape, 1)
    in_high = lanes >= BLOCK // 2
    mz = signed(grp_id * (BLOCK // 2) + jnp.where(in_high, lanes - BLOCK // 2, lanes))
    base_sq = mx * mx + mz * mz
    unit = 2.0 * math.pi / G * (2.0 * math.pi / G)
    for pair in range(width_y // 2):
        first = pl.ds(2 * pair, lines, stride=width_y)
        second = pl.ds(2 * pair + 1, lines, stride=width_y)
        one = data[first, :]
        two = data[second, :]
        even = jnp.where(low_half, one, pltpu.roll(two, BLOCK // 2, 1))
        odd = jnp.where(low_half, pltpu.roll(one, BLOCK // 2, 1), two)
        column = jnp.concatenate([even, odd], axis=0)
        spectrum = dot3(dot_nn, forward, split2(column))
        my = signed(dom_id * width_y + 2 * pair + in_high.astype(jnp.int32))
        squares = base_sq + my * my
        wave = squares.astype(F32) * unit
        safe = jnp.where(squares > 0, wave, 1.0)
        green = jnp.where(
            squares > 0, 4.0 * math.pi * jnp.exp(-wave / (4.0 * EWALD * EWALD)) / safe, 0.0
        ) * (1.0 / (G * G * G))
        result = dot3(dot_nn, back, split2(spectrum * green))
        even = result[:lines]
        odd = result[lines:]
        out[first, :] = jnp.where(low_half, even, pltpu.roll(odd, BLOCK // 2, 1))
        out[second, :] = jnp.where(low_half, pltpu.roll(even, BLOCK // 2, 1), odd)


def sample_kernel(local, frac, charge, energy, data, hz_hi, hz_lo, site, field, mesh_s):
    planes, padded_y, unused_z = mesh_s.shape
    groups = data.shape[0]
    window = 24
    tile = (G // groups) // TILES_Y
    low_half = lax.broadcasted_iota(jnp.int32, (padded_y, BLOCK), 1) < BLOCK // 2
    table = (hz_hi[...], hz_lo[...])
    for q in range(planes // 2):
        evens = []
        odds = []
        for h in range(groups // 2):
            one = data[2 * h, q]
            two = data[2 * h + 1, q]
            evens.append(jnp.where(low_half, one, pltpu.roll(two, BLOCK // 2, 1)))
            odds.append(jnp.where(low_half, pltpu.roll(one, BLOCK // 2, 1), two))
        both = jnp.concatenate(
            [jnp.concatenate(evens, axis=1), jnp.concatenate(odds, axis=1)], axis=0
        )
        mesh_s[2 * q : 2 * q + 2] = dot3(dot_nn, split2(both), table).reshape(2, padded_y, G)
    for t, pair in chunk_blocks(charge.shape[0]):
        lx, fx = lanes_of(local, 0, pair), lanes_of(frac, 0, pair)
        ly, fy = lanes_of(local, 1, pair), lanes_of(frac, 1, pair)
        lz, fz = lanes_of(local, 2, pair), lanes_of(frac, 2, pair)
        wx = spline_rows(planes, 0, lx, fx, False, False)
        sx = spline_rows(planes, 0, lx, fx, False, True)
        wy = spline_rows(window, tile * t, ly, fy, False, False)
        sy = spline_rows(window, tile * t, ly, fy, False, True)
        wz = spline_rows(G, 0, lz, fz, True, False)
        sz = spline_rows(G, 0, lz, fz, True, True)
        strip = split2(mesh_s[:, tile * t : tile * t + window, :].reshape(planes * window, G))
        along = dot3(dot_nn, strip, split2(wz))
        slope = dot3(dot_nn, strip, split2(sz))
        value_y = jnp.zeros_like(wy)
        grad_y = jnp.zeros_like(wy)
        slope_y = jnp.zeros_like(wy)
        for x in range(planes):
            here = along[x * window : (x + 1) * window]
            value_y = value_y + wx[x : x + 1] * here
            grad_y = grad_y + sx[x : x + 1] * here
            slope_y = slope_y + wx[x : x + 1] * slope[x * window : (x + 1) * window]
        pot = jnp.sum(wy * value_y, axis=0, keepdims=True)
        rows = [
            -jnp.sum(wy * grad_y, axis=0, keepdims=True),
            -jnp.sum(sy * value_y, axis=0, keepdims=True),
            -jnp.sum(wy * slope_y, axis=0, keepdims=True),
        ]
        result = rows_of(energy, pair) + 0.5 * rows_of(charge, pair) * pot
        for k, b in enumerate(pair):
            cut = slice(k * BLOCK, (k + 1) * BLOCK)
            site[b : b + 1, :] = result[:, cut]
            for c in range(3):
                field[c : c + 1, b * BLOCK : (b + 1) * BLOCK] = rows[c][:, cut]


VMEM_SPEC = pl.BlockSpec(memory_space=pltpu.VMEM)
SMEM_SPEC = pl.BlockSpec(memory_space=pltpu.SMEM)


def call(body, outs, scratch, scalars, args):
    specs = [SMEM_SPEC] * scalars + [VMEM_SPEC] * (len(args) - scalars)
    many = isinstance(outs, (list, tuple))
    return pl.pallas_call(
        body,
        out_shape=outs,
        in_specs=specs,
        out_specs=[VMEM_SPEC] * len(outs) if many else VMEM_SPEC,
        scratch_shapes=scratch,
        compiler_params=pltpu.CompilerParams(vmem_limit_bytes=VMEM_BYTES),
    )(*args)


def pair_call(
    pair_blocks, counts, left, record, right, species_embed, neighbour_embed, w_radial, w_hidden, w_charge, w_energy
):
    blocks = record.shape[1] // BLOCK
    width = w_charge.shape[0]
    shape = jax.ShapeDtypeStruct((blocks, BLOCK), F32)
    square = pltpu.VMEM((BLOCK, BLOCK), F32)
    return call(
        functools.partial(pair_kernel, step=4),
        [shape, shape],
        [
            pltpu.VMEM((record.shape[0], 3 * record.shape[1]), F32),
            pltpu.VMEM((width, BLOCK), BF),
            pltpu.VMEM((width, width), BF),
            *[square] * 4,
        ],
        2,
        (
            pair_blocks,
            counts,
            left,
            record,
            right,
            w_radial,
            species_embed,
            neighbour_embed,
            w_hidden,
            w_charge[None, :],
            w_energy[None, :],
        ),
    )


def tables(slab, quarter, doms, groups, padded_y):
    planes = slab + 2
    points = np.arange(G)
    plain = hartley(points)
    half = G // groups
    order = np.concatenate([np.tile(np.arange(s * half, (s + 1) * half), 2) for s in range(groups)])
    hz_dup = plain[order].T
    hz_inv = plain
    y_points = np.array([quarter * g - 1 + r for g in range(groups) for r in range(padded_y)]) % G
    y_used = np.array([r < quarter + 2 for g in range(groups) for r in range(padded_y)])
    hy = hartley(y_points) * y_used[None, :]
    x_points = np.array(
        [slab * d - 1 + 2 * q + par for par in range(2) for d in range(doms) for q in range(planes // 2)]
    ) % G
    hx = hartley(x_points)
    return [np_split(t) for t in (hz_dup, hz_inv, hy, hy.T, hx, hx.T)]


def on_device(
    cell_index,
    offsets,
    species,
    pair_blocks,
    counts,
    background,
    species_embed,
    neighbour_embed,
    w_radial,
    w_hidden,
    w_charge,
    w_energy,
):
    atoms = cell_index.shape[1]
    blocks = atoms // BLOCK
    doms = lax.axis_size("dom")
    groups = lax.axis_size("grp")
    slab = G // doms
    quarter = G // groups
    planes = slab + 2
    pairs = planes // 2
    padded_y = quarter + 8
    width_y = G // doms
    dom_id = lax.axis_index("dom")
    grp_id = lax.axis_index("grp")
    hz_dup, hz_inv, hy, hy_inv, hx, hx_inv = tables(slab, quarter, doms, groups, padded_y)

    positions = cell_index.astype(F32) + offsets
    record = jnp.concatenate([positions, species.astype(F32)[None, :]], axis=0)
    left = lax.ppermute(record, "dom", [(i, (i + 1) % doms) for i in range(doms)])
    right = lax.ppermute(record, "dom", [((i + 1) % doms, i) for i in range(doms)])
    energies, charges = pair_call(
        pair_blocks,
        counts,
        left,
        record,
        right,
        species_embed,
        neighbour_embed,
        w_radial,
        w_hidden,
        w_charge,
        w_energy,
    )

    origin = jnp.stack([1 - slab * dom_id, 1 - quarter * grp_id, jnp.zeros_like(dom_id)])
    local = cell_index + origin[:, None]
    spec = call(
        spread_kernel,
        jax.ShapeDtypeStruct((groups, pairs, padded_y, BLOCK), F32),
        [pltpu.VMEM((planes, padded_y, G), F32)],
        0,
        (local, offsets, charges, background, *hz_dup),
    )
    spec = hop_call(spec, hy, (doms, pairs, width_y, BLOCK), "grp", "dom", 0)
    place = jnp.stack([grp_id, dom_id]).astype(jnp.int32)
    spec = call(
        functools.partial(x_kernel, width_y=width_y),
        jax.ShapeDtypeStruct((doms * pairs * width_y, BLOCK), F32),
        [],
        1,
        (place, spec.reshape(doms * pairs * width_y, BLOCK), *hx, *hx_inv),
    )
    spec = spec.reshape(doms, pairs, width_y, BLOCK)
    spec = hop_call(spec, hy_inv, (groups, pairs, padded_y, BLOCK), "dom", "grp", 1)
    site, field = call(
        sample_kernel,
        [jax.ShapeDtypeStruct((blocks, BLOCK), F32), jax.ShapeDtypeStruct((3, atoms), F32)],
        [pltpu.VMEM((planes, padded_y, G), F32)],
        0,
        (local, offsets, charges, energies, spec, *hz_inv),
    )
    return (site.reshape(atoms), field, charges.reshape(atoms))


def solution(mesh):
    return jax.shard_map(
        on_device,
        mesh=mesh,
        in_specs=(
            P(None, ("grp", "dom")),
            P(None, ("grp", "dom")),
            P(("grp", "dom")),
            P(("grp", "dom"), None),
            P(("grp", "dom")),
            P("dom", "grp", None),
            P(),
            P(),
            P(),
            P(),
            P(),
            P(),
        ),
        out_specs=(P(("grp", "dom")), P(None, ("grp", "dom")), P(("grp", "dom"))),
        check_vma=False,
    )
```
